128 devices in a mesh: gx: 8 (over y, core), gy: 16 (over z, x).
Axes of the slice: x: 4, y: 4, z: 4, core: 2. Of those that a mesh axis runs over, the one named last changes fastest.
Arguments:
- flow_fields: float32 [6, 16, 512, 2048], P(None, None, 'gx', 'gy'), may hold values from -6 to 6
- cell_index: int32 [3, 131072], P(None, ('gx', 'gy')), may hold values from 0 to 127, as said below
- stencil_shift: int32 [3, 131072], P(None, ('gx', 'gy')), may hold values from -1 to 0
- fraction_in_cell: float32 [3, 131072], P(None, ('gx', 'gy')), may hold values from 0 to 1
- bubble_speed: float32 [3, 131072], P(None, ('gx', 'gy')), may hold values from -6 to 6
- history: float32 [3, 256, 131072], P(None, None, ('gx', 'gy')), may hold values from -4 to 4
- live_count: int32 [128], P(('gx', 'gy')), may hold values from 512 to 1024, as said below
- mig_slots: int32 [128, 8, 16], P(('gx', 'gy')), may hold values from 0 to 1023, as said below
- mig_count: int32 [128, 8], P(('gx', 'gy')), may hold values from 0 to 16, as said below
Outputs:
- new_speed: float32 [3, 131072], P(None, ('gx', 'gy'))
- new_position: float32 [3, 131072], P(None, ('gx', 'gy'))
- new_history: float32 [3, 256, 131072], P(None, None, ('gx', 'gy'))
- arrived_state: float32 [8, 6, 2048], P(None, None, ('gx', 'gy'))
- arrived_history: float32 [8, 3, 256, 2048], P(None, None, None, ('gx', 'gy'))
The draws below stay inside these ranges and needn't reach their ends.
Inputs may be any that keep to these rules, and one draw needn't show every extreme that they name: `cell_index`: each component lies in its tile: x below 64, y below 128, z below 16. `live_count`: at least half of 1024 and at least 128; some tile is full. `mig_slots`: the used entries of a tile's 8 lists are distinct live slots of that tile; entries past the count are slots too and are ignored. `mig_count`: some list is full in every draw.
All inputs are finite; a program needn't handle non-finite values.
Results may differ from the reference program's by a relative error of at most 0.0003.
Values sent between devices are 32-bit elements; how exact they have to be, the bound alone decides.
No kernel may reach another device: no remote copies, remote signals or barrier semaphores. Data moves between devices by JAX's collectives and lax.ppermute only.
A program may use at most 192 MiB of HBM per device.

```python
import jax
import jax.numpy as jnp
from jax import lax

CX = 64
CY = 128
NZ = 16
NB = 1024
CAP = 16
H = 256
NX = 512
NY = 2048
TILES = 128
BUB = 131072
ARR = 2048
N_GX = 8
N_GY = 16


def tile_loads(key):
    base = jax.random.fold_in(key, 4242)
    lowest = max(8 * CAP, NB // 2)
    live = jax.random.randint(jax.random.fold_in(base, 1), (TILES,), lowest, NB + 1, dtype=jnp.int32)
    full = jax.random.randint(jax.random.fold_in(base, 2), (), 0, TILES, dtype=jnp.int32)
    other = (full + 1 + jax.random.randint(jax.random.fold_in(base, 3), (), 0, TILES - 1, dtype=jnp.int32)) % TILES
    live = live.at[other].set(lowest)
    live = live.at[full].set(NB)
    return live


def draw_live_count(key, part):
    return tile_loads(key)


def draw_mig_slots(key, part):
    live = tile_loads(key)
    base = jax.random.fold_in(key, 777)

    def one_tile(tile, limit):
        perm = jax.random.permutation(jax.random.fold_in(base, tile), NB).astype(jnp.int32)
        order = jnp.argsort(jnp.where(perm < limit, 0, 1).astype(jnp.int32), stable=True)
        return perm[order][:8 * CAP].reshape(8, CAP)
    return jax.vmap(one_tile)(jnp.arange(TILES, dtype=jnp.int32), live)


def draw_mig_count(key, part):
    base = jax.random.fold_in(key, 913)
    counts = jax.random.randint(jax.random.fold_in(base, 1), (TILES * 8,), 0, CAP + 1, dtype=jnp.int32)
    spot = jax.random.randint(jax.random.fold_in(base, 2), (), 0, TILES * 8, dtype=jnp.int32)
    return counts.at[spot].set(CAP).reshape(TILES, 8)


def draw_cell_index(key, part):
    base = jax.random.fold_in(key, 31)
    cell_x = jax.random.randint(jax.random.fold_in(base, 1), (TILES * NB,), 0, CX, dtype=jnp.int32)
    cell_y = jax.random.randint(jax.random.fold_in(base, 2), (TILES * NB,), 0, CY, dtype=jnp.int32)
    cell_z = jax.random.randint(jax.random.fold_in(base, 3), (TILES * NB,), 0, NZ, dtype=jnp.int32)
    return jnp.stack([cell_x, cell_y, cell_z])


def plant(entries, key, low, high):
    longest = entries.shape.index(max(entries.shape))
    spots = []
    for shift in (0, 1):
        where = [jax.random.randint(jax.random.fold_in(key, axis), (), 0, length) for axis, length in enumerate(entries.shape)]
        where[longest] = (where[longest] + shift) % entries.shape[longest]
        spots.append(tuple(where))
    return entries.at[spots[0]].set(low).at[spots[1]].set(high)


def level_of(key, extent, shards, smallest, high):
    def one(dim, blocks):
        heights = jax.random.uniform(jax.random.fold_in(jax.random.fold_in(key, 6), dim), (blocks,), jnp.float32, smallest / len(shards), high / len(shards))
        return jnp.repeat(jnp.exp(heights), extent[dim] // blocks).reshape((-1,) + (1,) * (len(extent) - dim - 1))

    loudness = one(*shards[0])
    for cut in shards[1:]:
        loudness = loudness * one(*cut)
    return loudness


def scatter_about(own_key, extent, deviation, bound, pieces=(), kind=jnp.bfloat16):
    entries = deviation * jax.random.normal(own_key, extent, jnp.float32)
    if pieces:
        entries = entries * level_of(own_key, extent, pieces, -0.22, 0.18)
    return jnp.clip(entries, -bound, bound).astype(kind)


def setup_inputs(seed: int = 0) -> dict:
    key_of = jax.random.split(jax.random.key(seed), 10)
    return {
        "flow_fields": scatter_about(key_of[0], (6, NZ, NX, NY), 1.0, 6.0, ((2, 8), (3, 16)), jnp.float32),
        "cell_index": draw_cell_index(jax.random.fold_in(key_of[9], 71), 0),
        "stencil_shift": plant(jax.random.randint(key_of[2], (3, BUB), -1, 1), jax.random.fold_in(key_of[2], 1), -1, 0).astype(jnp.int32),
        "fraction_in_cell": jnp.clip(1.0 * jax.random.uniform(key_of[3], (3, BUB), jnp.float32) ** level_of(key_of[3], (3, BUB), ((1, 128),), -0.2, 0.2), 0.0, 1.0),
        "bubble_speed": scatter_about(key_of[4], (3, BUB), 1.0, 6.0, ((1, 128),), jnp.float32),
        "history": scatter_about(key_of[5], (3, H, BUB), 0.5, 4.0, ((2, 128),), jnp.float32),
        "live_count": draw_live_count(jax.random.fold_in(key_of[9], 71), 0),
        "mig_slots": draw_mig_slots(jax.random.fold_in(key_of[9], 71), 0),
        "mig_count": draw_mig_count(jax.random.fold_in(key_of[9], 71), 0),
    }


neighbours = ((-1, -1), (-1, 0), (-1, 1), (0, -1), (0, 1), (1, -1), (1, 0), (1, 1))
step_dt = 0.1
relax_tau = 0.5
basset_coef = 0.3

def lagrange_basis(s):
    return jnp.stack([-s * (s - 1.0) * (s - 2.0) / 6.0, (s + 1.0) * (s - 1.0) * (s - 2.0) / 2.0, -(s + 1.0) * s * (s - 2.0) / 2.0, (s + 1.0) * s * (s - 1.0) / 6.0])

def advance(fluid_field, speed, fraction_part, history, alive):
    steps_h = history.shape[1]
    karg = jnp.arange(1, steps_h + 1, dtype=jnp.float32)
    quad = jnp.sqrt(karg + 1.0) - jnp.sqrt(karg)
    tail = jnp.einsum('ckb,k->cb', history, quad, precision=lax.Precision.HIGHEST)
    fluid_u = fluid_field[0:3]
    fluid_a = fluid_field[3:6]

    def rate(v):
        return 3.0 * fluid_a + (fluid_u - v) / relax_tau + basset_coef * (fluid_u - v + tail)
    v1 = speed + step_dt * rate(speed)
    v2 = 0.75 * speed + 0.25 * (v1 + step_dt * rate(v1))
    vn = speed / 3.0 + 2.0 / 3.0 * (v2 + step_dt * rate(v2))
    posn = fraction_part + step_dt * (speed / 6.0 + v1 / 6.0 + 2.0 * v2 / 3.0)
    hist_new = jnp.concatenate([(fluid_u - vn)[:, None, :], history[:, :steps_h - 1, :]], axis=1)
    keep = alive.astype(jnp.float32)
    return (vn * keep, posn * keep, hist_new * keep)

def reference(flow_fields, cell_index, stencil_shift, fraction_in_cell, bubble_speed, history, live_count, mig_slots, mig_count):
    flow_flat = flow_fields.reshape(6, NZ * NX * NY)
    nodes = jnp.arange(-1, 3, dtype=jnp.int32)

    def per_tile(inputs):
        tile, cells, offset_values, fraction_part, speed, hist, live, slots, counts = inputs
        row_i = tile // N_GY
        row_j = tile % N_GY
        bx = row_i * CX + cells[0] + offset_values[0]
        by = row_j * CY + cells[1] + offset_values[1]
        bz = cells[2] + offset_values[2]
        xs = (bx[None, :] + nodes[:, None]) % NX
        ys = (by[None, :] + nodes[:, None]) % NY
        zs = (bz[None, :] + nodes[:, None]) % NZ
        sampled_value = fraction_part - offset_values.astype(jnp.float32)
        weight_along_x = lagrange_basis(sampled_value[0])
        weight_along_y = lagrange_basis(sampled_value[1])
        weight_along_z = lagrange_basis(sampled_value[2])
        idx = (zs[:, None, None, :] * (NX * NY) + xs[None, :, None, :] * NY + ys[None, None, :, :]).reshape(64, -1)
        combined_weight = (weight_along_z[:, None, None, :] * weight_along_x[None, :, None, :] * weight_along_y[None, None, :, :]).reshape(64, -1)
        selected_samples = flow_flat[:, idx]
        fluid_field = jnp.einsum('rey,ey->ry', selected_samples, combined_weight, precision=lax.Precision.HIGHEST)
        alive = jnp.arange(NB, dtype=jnp.int32) < live
        vn, posn, hist_new = advance(fluid_field, speed, fraction_part, hist, alive)
        state = jnp.concatenate([vn, posn], axis=0)
        used = (jnp.arange(CAP, dtype=jnp.int32)[None, :] < counts[:, None]).astype(jnp.float32)
        out_state = jnp.transpose(state[:, slots], (1, 0, 2)) * used[:, None, :]
        out_hist = jnp.transpose(hist_new[:, :, slots], (2, 0, 1, 3)) * used[:, None, None, :]
        return (vn, posn, hist_new, out_state, out_hist)

    def tiles_first(a):
        return jnp.moveaxis(a.reshape(a.shape[:-1] + (TILES, NB)), -2, 0)
    tile_ids = jnp.arange(TILES, dtype=jnp.int32)
    vn, posn, hist_new, out_state, out_hist = lax.map(per_tile, (tile_ids, tiles_first(cell_index), tiles_first(stencil_shift), tiles_first(fraction_in_cell), tiles_first(bubble_speed), tiles_first(history), live_count, mig_slots, mig_count))
    new_speed = jnp.transpose(vn, (1, 0, 2)).reshape(3, BUB)
    new_position = jnp.transpose(posn, (1, 0, 2)).reshape(3, BUB)
    new_history = jnp.transpose(hist_new, (1, 2, 0, 3)).reshape(3, H, BUB)
    row_i = tile_ids // N_GY
    row_j = tile_ids % N_GY
    state_list = []
    hist_list = []
    for d, (dx, dy) in enumerate(neighbours):
        source = (row_i - dx) % N_GX * N_GY + (row_j - dy) % N_GY
        state_list.append(jnp.transpose(out_state[source, d], (1, 0, 2)).reshape(6, ARR))
        hist_list.append(jnp.transpose(out_hist[source, d], (1, 2, 0, 3)).reshape(3, H, ARR))
    return (new_speed, new_position, new_history, jnp.stack(state_list), jnp.stack(hist_list))
```

```python
import jax
import jax.numpy as jnp
from jax import lax
from jax.experimental import pallas as pl
from jax.experimental.pallas import tpu as pltpu
from jax.sharding import PartitionSpec as P

step_dt = 0.1
relax_tau = 0.5
basset_coef = 0.3

CX, CY, NZ, NB, CAP, H = 64, 128, 16, 1024, 16, 256
NF = 6
SLOTS = 8 * CAP
LANES = 256
f32 = jnp.float32
bf16 = jnp.bfloat16
VMEM = pl.BlockSpec(memory_space=pltpu.VMEM)
HBM = pl.BlockSpec(memory_space=pl.ANY)


def shape(dims, dtype=f32):
    return jax.ShapeDtypeStruct(dims, dtype)


def split(value):
    high = value.astype(bf16)
    return high, (value - high.astype(f32)).astype(bf16)


def mul(a, b):
    return jnp.dot(a, b, preferred_element_type=f32)


def rows_of(dims):
    return lax.broadcasted_iota(jnp.int32, dims, 0)


def from_behind(value, axis, steps):
    count = lax.axis_size(axis)
    return lax.ppermute(value, axis, [(k, (k + steps) % count) for k in range(count)])


def basis(s):
    return (
        -s * (s - 1.0) * (s - 2.0) / 6.0,
        (s + 1.0) * (s - 1.0) * (s - 2.0) / 2.0,
        -(s + 1.0) * s * (s - 2.0) / 2.0,
        (s + 1.0) * s * (s - 1.0) / 6.0,
    )


def spread(offset, weights):
    out = jnp.zeros(offset.shape, f32)
    for node, weight in enumerate(weights):
        out = jnp.where(offset == node, weight, out)
    return out


def turn_kernel(field, high, low, first, last, buf, sems):
    copies = [pltpu.make_async_copy(field.at[c], buf.at[c], sems.at[c]) for c in range(NF)]
    for copy in copies:
        copy.start()
    first[...] = jnp.zeros(first.shape, f32)
    last[...] = jnp.zeros(last.shape, f32)
    for c in range(NF):
        copies[c].wait()
        turned = buf[c].T
        h, l = split(turned)
        high[c * CY : (c + 1) * CY, :] = h
        low[c * CY : (c + 1) * CY, :] = l
        for i in range(2):
            first[8 * i + c : 8 * i + c + 1, :] = turned[i : i + 1, :]
            last[8 * i + c : 8 * i + c + 1, :] = turned[CY - 2 + i : CY - 1 + i, :]


def turn(field):
    return pl.pallas_call(
        turn_kernel,
        out_shape=(
            shape((NF * CY, NZ * CX), bf16),
            shape((NF * CY, NZ * CX), bf16),
            shape((16, NZ * CX)),
            shape((16, NZ * CX)),
        ),
        in_specs=[HBM],
        out_specs=(VMEM,) * 4,
        scratch_shapes=[pltpu.VMEM((NF, NZ * CX, CY), f32), pltpu.SemaphoreType.DMA((NF,))],
        compiler_params=pltpu.CompilerParams(vmem_limit_bytes=20 << 20),
        cost_estimate=pl.CostEstimate(flops=0, bytes_accessed=9 << 20, transcendentals=0),
        name="turn",
    )(field)


def edge_kernel(below, above, first, last, stacked, send_first, send_last):
    send_first[...] = jnp.zeros(send_first.shape, f32)
    send_last[...] = jnp.zeros(send_last.shape, f32)
    send_first[:, : NZ * CX] = first[...]
    send_last[:, : NZ * CX] = last[...]
    for c in range(NF):
        block = jnp.concatenate(
            [below[32 * c : 32 * c + 32, :], above[32 * c : 32 * c + 32, :], jnp.zeros((64, CY), f32)], axis=0
        )
        turned = block.T
        high = turned.astype(bf16).astype(f32)
        low = turned - high
        stacked[c * CY : (c + 1) * CY, :128] = (high + pltpu.roll(low, 64, 1)).astype(bf16)
        stacked[c * CY : (c + 1) * CY, 128:] = high.astype(bf16)
        for i in range(2):
            send_first[8 * i + c : 8 * i + c + 1, NZ * CX :] = turned[i : i + 1, :]
            send_last[8 * i + c : 8 * i + c + 1, NZ * CX :] = turned[CY - 2 + i : CY - 1 + i, :]


def edge(below, above, first, last):
    return pl.pallas_call(
        edge_kernel,
        out_shape=(shape((NF * CY, 256), bf16), shape((16, NZ * CX + 128)), shape((16, NZ * CX + 128))),
        in_specs=[VMEM] * 4,
        out_specs=(VMEM,) * 3,
        cost_estimate=pl.CostEstimate(flops=0, bytes_accessed=1 << 20, transcendentals=0),
        name="edge",
    )(below, above, first, last)


def past_kernel(live, hist, cell, shift, frac, speed, slots, used, new_hist, head, facts, moved, gone, buf, out, sems, osems):
    copies = [pltpu.make_async_copy(hist.at[c], buf.at[c], sems.at[c]) for c in range(3)]
    for copy in copies:
        copy.start()
    keep = (lax.broadcasted_iota(jnp.int32, (1, NB), 1) < live[0]).astype(f32)
    facts[...] = jnp.zeros(facts.shape, f32)
    facts[0:3, :] = (cell[...] + shift[...]).astype(f32)
    facts[8:11, :] = frac[...] - shift[...].astype(f32)
    facts[16:19, :] = frac[...]
    facts[24:27, :] = speed[...]
    facts[40:41, :] = keep
    choose = jnp.where(
        (lax.broadcasted_iota(jnp.int32, (NB, SLOTS), 0) == slots[...]) & (used[...] > 0), 1.0, 0.0
    ).astype(bf16)
    karg = (rows_of((H, 128)) + 1).astype(f32)
    quad = jnp.sqrt(karg + 1.0) - jnp.sqrt(karg)
    quad = jnp.concatenate([quad] * (NB // 128), axis=1)
    top = rows_of((H, NB)) == 0

    def pick(value):
        a = value.astype(bf16)
        rest = value - a.astype(f32)
        b = rest.astype(bf16)
        c = (rest - b.astype(f32)).astype(bf16)
        return mul(a, choose) + mul(b, choose) + mul(c, choose)

    outs = []
    for c in range(3):
        copies[c].wait()
        past = buf[c]
        facts[32 + c : 33 + c, :] = jnp.sum(past * quad, axis=0, keepdims=True)
        shifted = jnp.where(top, 0.0, pltpu.roll(past, 1, 0)) * keep
        out[c] = shifted
        outs.append(pltpu.make_async_copy(out.at[c], new_hist.at[c], osems.at[c]))
        outs[c].start()
        head[c] = shifted[0:8, :]
        moved[:, c] = pick(shifted).T.reshape(8, CAP, H)
    gone[...] = pick(facts[...])
    for copy in outs:
        copy.wait()


def past(live, hist, cell, shift, frac, speed, slots, used):
    return pl.pallas_call(
        past_kernel,
        out_shape=(
            shape((3, H, NB)),
            shape((3, 8, NB)),
            shape((48, NB)),
            shape((8, 3, CAP, H)),
            shape((48, SLOTS)),
        ),
        in_specs=[pl.BlockSpec(memory_space=pltpu.SMEM), HBM] + [VMEM] * 6,
        out_specs=(HBM,) + (VMEM,) * 4,
        scratch_shapes=[
            pltpu.VMEM((3, H, NB), f32),
            pltpu.VMEM((3, H, NB), f32),
            pltpu.SemaphoreType.DMA((3,)),
            pltpu.SemaphoreType.DMA((3,)),
        ],
        compiler_params=pltpu.CompilerParams(vmem_limit_bytes=24 << 20),
        cost_estimate=pl.CostEstimate(flops=600_000_000, bytes_accessed=8 << 20, transcendentals=0),
        name="past",
    )(live, hist, cell, shift, frac, speed, slots, used)


def flow_at(facts, high, low, stacked, ya, yb, wh, wl):
    n = facts.shape[1]
    base = facts[0:3, :].astype(jnp.int32)
    wx = [w[0:1] for w in basis(facts[8:9, :])]
    wy = [w[0:1] for w in basis(facts[9:10, :])]
    wz = [w[0:1] for w in basis(facts[10:11, :])]
    bx, by, bz = base[0:1], base[1:2], base[2:3]
    along_x = spread(rows_of((CX, n)) - bx + 1, wx)
    along_y = spread(rows_of((CY, n)) - by + 1, wy)
    along_z = spread((rows_of((NZ, n)) - bz + 1) & (NZ - 1), wz)
    for z in range(NZ):
        h, l = split(along_x * along_z[z : z + 1, :])
        wh[z * CX : (z + 1) * CX, :n] = h
        wl[z * CX : (z + 1) * CX, :n] = l
    r = rows_of((2 * NZ, n))
    pair_z = spread(((r >> 1) - bz + 1) & (NZ - 1), wz)
    side = jnp.concatenate(
        [pair_z * spread((r & 1) - 2 - bx + 1, wx), pair_z * spread((r & 1) + CX - bx + 1, wx)], axis=0
    )
    h, l = split(side)
    side = jnp.concatenate([h, h, l, jnp.zeros((64, n), bf16)], axis=0)
    w_h, w_l = wh[:, :n], wl[:, :n]
    total = mul(high[...], w_h) + mul(low[...], w_h) + mul(high[...], w_l) + mul(stacked[...], side)
    fluid = [
        jnp.sum(total[c * CY : (c + 1) * CY, :] * along_y, axis=0, keepdims=True) for c in range(NF)
    ]
    ends = jnp.concatenate([ya[...], yb[...]], axis=0)
    inner_h, inner_l = split(ends[:, : NZ * CX])
    outer = ends[:, NZ * CX :]
    outer_h = outer.astype(bf16).astype(f32)
    outer = jnp.concatenate([outer_h + pltpu.roll(outer - outer_h, 64, 1), outer_h], axis=1).astype(bf16)
    rim = mul(inner_h, w_h) + mul(inner_l, w_h) + mul(inner_h, w_l) + mul(outer, side)
    extra = jnp.zeros((8, n), f32)
    for k, y in enumerate((-2, -1, CY, CY + 1)):
        extra = extra + rim[8 * k : 8 * k + 8, :] * spread(y - by + 1, wy)
    u = jnp.concatenate(fluid[0:3], axis=0) + extra[0:3]
    a = jnp.concatenate(fluid[3:6], axis=0) + extra[3:6]
    return u, a


def advance(facts, u, a):
    frac, speed, tail, keep = facts[16:19, :], facts[24:27, :], facts[32:35, :], facts[40:41, :]

    def rate(v):
        return 3.0 * a + (u - v) / relax_tau + basset_coef * (u - v + tail)

    v1 = speed + step_dt * rate(speed)
    v2 = 0.75 * speed + 0.25 * (v1 + step_dt * rate(v1))
    vn = speed / 3.0 + 2.0 / 3.0 * (v2 + step_dt * rate(v2))
    posn = frac + step_dt * (speed / 6.0 + v1 / 6.0 + 2.0 * v2 / 3.0)
    return vn * keep, posn * keep, (u - vn) * keep


def leaving_kernel(facts, high, low, stacked, ya, yb, late, wh, wl):
    u, a = flow_at(facts, high, low, stacked, ya, yb, wh, wl)
    vn, posn, recent = advance(facts, u, a)
    late[...] = jnp.zeros(late.shape, f32)
    late[0:3, :] = vn
    late[3:6, :] = posn
    late[6:9, :] = recent


def leaving(facts, high, low, stacked, ya, yb):
    return pl.pallas_call(
        leaving_kernel,
        out_shape=shape((16, SLOTS)),
        in_specs=[VMEM] * 6,
        out_specs=VMEM,
        scratch_shapes=[pltpu.VMEM((NZ * CX, SLOTS), bf16)] * 2,
        compiler_params=pltpu.CompilerParams(vmem_limit_bytes=20 << 20),
        cost_estimate=pl.CostEstimate(flops=1_000_000_000, bytes_accessed=4 << 20, transcendentals=0),
        name="leaving",
    )(facts, high, low, stacked, ya, yb)


def staying_kernel(facts, high, low, stacked, ya, yb, head, hist_in, vel, pos, hist_out, wh, wl, rows, sem):
    del hist_in

    @pl.loop(0, NB // LANES)
    def _(tile):
        lanes = pl.ds(pl.multiple_of(tile * LANES, LANES), LANES)
        mine = facts[:, lanes]
        u, a = flow_at(mine, high, low, stacked, ya, yb, wh, wl)
        vn, posn, recent = advance(mine, u, a)
        vel[:, lanes] = vn
        pos[:, lanes] = posn
        for c in range(3):
            rows[c, :, lanes] = head[c, :, lanes]
            rows[c, 0:1, lanes] = recent[c : c + 1]

    copy = pltpu.make_async_copy(rows, hist_out.at[:, pl.ds(0, 8), :], sem)
    copy.start()
    copy.wait()


def staying(facts, high, low, stacked, ya, yb, head, hist):
    return pl.pallas_call(
        staying_kernel,
        out_shape=(shape((3, NB)), shape((3, NB)), shape((3, H, NB))),
        in_specs=[VMEM] * 7 + [HBM],
        out_specs=(VMEM, VMEM, HBM),
        scratch_shapes=[
            pltpu.VMEM((NZ * CX, LANES), bf16),
            pltpu.VMEM((NZ * CX, LANES), bf16),
            pltpu.VMEM((3, 8, NB), f32),
            pltpu.SemaphoreType.DMA,
        ],
        input_output_aliases={7: 2},
        compiler_params=pltpu.CompilerParams(vmem_limit_bytes=20 << 20),
        cost_estimate=pl.CostEstimate(flops=6_000_000_000, bytes_accessed=4 << 20, transcendentals=0),
        name="staying",
    )(facts, high, low, stacked, ya, yb, head, hist)


def on_device(flow, cell, shift, frac, speed, hist, live, mig_slots, mig_count):
    below = from_behind(flow[:, :, CX - 2 :, :].reshape(NF * NZ * 2, CY), "gx", 1)
    above = from_behind(flow[:, :, :2, :].reshape(NF * NZ * 2, CY), "gx", -1)
    high, low, first, last = turn(flow.reshape(NF, NZ * CX, CY))
    stacked, send_first, send_last = edge(below, above, first, last)
    ya = from_behind(send_last, "gy", 1)
    yb = from_behind(send_first, "gy", -1)

    used = (lax.broadcasted_iota(jnp.int32, (8, CAP), 1) < mig_count.reshape(8, 1)).astype(jnp.int32)
    used = used.reshape(1, SLOTS)
    new_hist, head, facts, moved, gone = past(
        live, hist, cell, shift, frac, speed, mig_slots.reshape(1, SLOTS), used
    )
    gone = gone.at[40:41, :].set(used.astype(f32))

    late = leaving(gone, high, low, stacked, ya, yb)
    vel, pos, new_hist = staying(facts, high, low, stacked, ya, yb, head, new_hist)

    def travel(own, pick):
        fore = from_behind(own if pick is None else own[5:8], "gx", 1)
        back = from_behind(own if pick is None else own[0:3], "gx", -1)
        return fore, back

    fore, back = travel(moved, True)
    up = from_behind(jnp.stack([back[2], moved[4], fore[2]]), "gy", 1)
    down = from_behind(jnp.stack([back[0], moved[3], fore[0]]), "gy", -1)
    bulk = jnp.stack([down[0], back[1], up[0], down[1], up[1], down[2], fore[1], up[2]])

    fore, back = travel(late, None)
    which = lax.broadcasted_iota(jnp.int32, (16, SLOTS), 1) // CAP
    mixed = jnp.where(which < 3, back, jnp.where(which < 5, late, fore))
    up = from_behind(mixed, "gy", 1)
    down = from_behind(mixed, "gy", -1)
    side = jnp.where(which == 1, back, fore)
    upward = (which == 2) | (which == 4) | (which == 7)
    landed = jnp.where((which == 1) | (which == 6), side, jnp.where(upward, up, down))
    landed = landed.reshape(16, 8, CAP)
    arrived_state = jnp.transpose(landed[0:6], (1, 0, 2))
    recent = jnp.transpose(landed[6:9], (1, 0, 2))
    newest = lax.broadcasted_iota(jnp.int32, (8, 3, CAP, H), 3) == 0
    arrived_history = jnp.where(newest, recent[..., None], bulk)
    return vel, pos, new_hist, arrived_state, jnp.transpose(arrived_history, (0, 1, 3, 2))


def solution(mesh):
    both = ("gx", "gy")
    return jax.shard_map(
        on_device,
        mesh=mesh,
        in_specs=(
            P(None, None, "gx", "gy"),
            P(None, both),
            P(None, both),
            P(None, both),
            P(None, both),
            P(None, None, both),
            P(both),
            P(both, None, None),
            P(both, None),
        ),
        out_specs=(P(None, both), P(None, both), P(None, None, both), P(None, None, both), P(None, None, None, both)),
        check_vma=False,
    )
```

```python
import functools

import jax
import jax.numpy as jnp
from jax import lax
from jax.experimental import pallas as pl
from jax.experimental.pallas import tpu as pltpu
from jax.sharding import PartitionSpec as P

step_dt = 0.1
relax_tau = 0.5
basset_coef = 0.3

CX, CY, NZ, NB, CAP, H = 64, 128, 16, 1024, 16, 256
NF = 6
SLOTS = 8 * CAP
LANES = 256
f32 = jnp.float32
bf16 = jnp.bfloat16
VMEM = pl.BlockSpec(memory_space=pltpu.VMEM)
HBM = pl.BlockSpec(memory_space=pltpu.HBM)
SMEM = pl.BlockSpec(memory_space=pltpu.SMEM)
INNER = NZ * CX
RIM = 16 * (INNER // 128 + 1)
REC = 2 * 3 * CAP
UP, DOWN, FORE, BACK = (2, 4, 7), (0, 3, 5), (5, 6, 7), (0, 1, 2)


def shape(dims, dtype=f32):
    return jax.ShapeDtypeStruct(dims, dtype)


def split(value):
    high = value.astype(bf16)
    return high, (value - high.astype(f32)).astype(bf16)


def mul(a, b):
    return jnp.dot(a, b, preferred_element_type=f32)


def rows_of(dims):
    return lax.broadcasted_iota(jnp.int32, dims, 0)


def from_behind(value, axis, steps):
    count = lax.axis_size(axis)
    return lax.ppermute(value, axis, [(k, (k + steps) % count) for k in range(count)])


def params(megabytes):
    return pltpu.CompilerParams(vmem_limit_bytes=megabytes << 20)


def outside(*arrays):
    return [pltpu.with_memory_space_constraint(x, pltpu.HBM) for x in arrays]


def cost(flops, megabytes):
    return pl.CostEstimate(flops=flops, bytes_accessed=int(megabytes * (1 << 20)), transcendentals=0)


def basis(s):
    return (
        -s * (s - 1.0) * (s - 2.0) / 6.0,
        (s + 1.0) * (s - 1.0) * (s - 2.0) / 2.0,
        -(s + 1.0) * s * (s - 2.0) / 2.0,
        (s + 1.0) * s * (s - 1.0) / 6.0,
    )


def spread(offset, weights):
    out = jnp.zeros(offset.shape, f32)
    for node, weight in enumerate(weights):
        out = jnp.where(offset == node, weight, out)
    return out


def prepare_kernel(
    live, field, hist, cell, shift, frac, speed, slots, counts_in,
    high, low, first, last, facts, moved, gone,
    fbuf, hbuf, ibuf, vbuf, sbuf, counts, fsem, hsem, isem,
):
    small = [
        pltpu.make_async_copy(src, dst, isem.at[k])
        for k, (src, dst) in enumerate(
            (
                (cell, ibuf.at[0]),
                (shift, ibuf.at[1]),
                (frac, vbuf.at[0]),
                (speed, vbuf.at[1]),
                (slots, sbuf),
                (counts_in, counts),
            )
        )
    ]
    fields = [pltpu.make_async_copy(field.at[c], fbuf.at[c], fsem.at[c]) for c in range(NF)]
    pasts = [pltpu.make_async_copy(hist.at[c], hbuf.at[c], hsem.at[c]) for c in range(3)]
    for copy in small + fields + pasts:
        copy.start()
    facts[...] = jnp.zeros(facts.shape, f32)
    first[...] = jnp.zeros(first.shape, f32)
    last[...] = jnp.zeros(last.shape, f32)
    for copy in small:
        copy.wait()
    lane = lax.broadcasted_iota(jnp.int32, (1, SLOTS), 1)
    used = jnp.zeros((1, SLOTS), f32)
    for d in range(8):
        used = jnp.where((lane >= d * CAP) & (lane < d * CAP + counts[0, d]), 1.0, used)
    offset = ibuf[1].astype(f32)
    facts[0:3, :] = (ibuf[0] + ibuf[1]).astype(f32)
    facts[8:11, :] = vbuf[0] - offset
    facts[16:19, :] = vbuf[0]
    facts[24:27, :] = vbuf[1]
    facts[40:41, :] = (lax.broadcasted_iota(jnp.int32, (1, NB), 1) < live[0]).astype(f32)
    listed = jnp.concatenate([sbuf[0].astype(f32), jnp.zeros((8, SLOTS - CAP), f32)], axis=1)
    place = jnp.zeros((1, SLOTS), f32)
    for d in range(8):
        row = listed[d : d + 1, :]
        place = place + (pltpu.roll(row, d * CAP, 1) if d else row)
    place = jnp.where(used > 0.0, place, -1.0).astype(jnp.int32)
    choose = jnp.where(lax.broadcasted_iota(jnp.int32, (NB, SLOTS), 0) == place, 1.0, 0.0).astype(bf16)

    def pick(value):
        a = value.astype(bf16)
        rest = value - a.astype(f32)
        b = rest.astype(bf16)
        c = (rest - b.astype(f32)).astype(bf16)
        return mul(a, choose) + mul(b, choose) + mul(c, choose)

    for c in range(NF):
        fields[c].wait()
        turned = fbuf[c].T
        h, l = split(turned)
        high[c * CY : (c + 1) * CY, :] = h
        low[c * CY : (c + 1) * CY, :] = l
        for i in range(2):
            first[8 * i + c : 8 * i + c + 1, :] = turned[i : i + 1, :]
            last[8 * i + c : 8 * i + c + 1, :] = turned[CY - 2 + i : CY - 1 + i, :]
    karg = (rows_of((H, 128)) + 1).astype(f32)
    quad = jnp.sqrt(karg + 1.0) - jnp.sqrt(karg)
    newest = lax.broadcasted_iota(jnp.int32, (SLOTS, H), 1) == 0
    for c in range(3):
        pasts[c].wait()
        for k in range(NB // 128):
            facts[32 + c : 33 + c, 128 * k : 128 * k + 128] = jnp.sum(
                hbuf[c, :, 128 * k : 128 * k + 128] * quad, axis=0, keepdims=True
            )
        chosen = jnp.where(newest, 0.0, pltpu.roll(pick(hbuf[c]).T, 1, 1))
        for half in range(2):
            moved[:, half, c] = chosen[:, 128 * half : 128 * half + 128].reshape(8, CAP, 128)
    gone[...] = pick(facts[...])
    gone[40:41, :] = used


def prepare(live, *arrays):
    return pl.pallas_call(
        prepare_kernel,
        out_shape=(
            shape((NF * CY, INNER), bf16),
            shape((NF * CY, INNER), bf16),
            shape((16, INNER)),
            shape((16, INNER)),
            shape((48, NB)),
            shape((8, 2, 3, CAP, 128)),
            shape((48, SLOTS)),
        ),
        in_specs=[SMEM] + [HBM] * 8,
        out_specs=(VMEM,) * 7,
        scratch_shapes=[
            pltpu.VMEM((NF, INNER, CY), f32),
            pltpu.VMEM((3, H, NB), f32),
            pltpu.VMEM((2, 3, NB), jnp.int32),
            pltpu.VMEM((2, 3, NB), f32),
            pltpu.VMEM((1, 8, CAP), jnp.int32),
            pltpu.SMEM((1, 8), jnp.int32),
            pltpu.SemaphoreType.DMA((NF,)),
            pltpu.SemaphoreType.DMA((3,)),
            pltpu.SemaphoreType.DMA((6,)),
        ],
        compiler_params=params(24),
        cost_estimate=cost(700_000_000, 10),
        name="prepare",
    )(live, *outside(*arrays))


def edge_kernel(below, above, first, last, moved, stacked, up, down):
    for out, row, which in ((up, last, UP), (down, first, DOWN)):
        for k in range(INNER // 128):
            out[16 * k : 16 * k + 16, :] = row[:, 128 * k : 128 * k + 128]
        out[RIM - 16 : RIM, :] = jnp.zeros((16, 128), f32)
        for k, d in enumerate(which):
            out[RIM + REC * k : RIM + REC * k + REC, :] = moved[d].reshape(REC, 128)
    for c in range(NF):
        block = jnp.concatenate(
            [below[32 * c : 32 * c + 32, :], above[32 * c : 32 * c + 32, :], jnp.zeros((64, CY), f32)], axis=0
        )
        turned = block.T
        h = turned.astype(bf16).astype(f32)
        stacked[c * CY : (c + 1) * CY, :128] = (h + pltpu.roll(turned - h, 64, 1)).astype(bf16)
        stacked[c * CY : (c + 1) * CY, 128:] = h.astype(bf16)
        for i in range(2):
            row = RIM - 16 + 8 * i + c
            down[row : row + 1, :] = turned[i : i + 1, :]
            up[row : row + 1, :] = turned[CY - 2 + i : CY - 1 + i, :]


def edge(below, above, first, last, moved):
    return pl.pallas_call(
        edge_kernel,
        out_shape=(shape((NF * CY, 256), bf16), shape((RIM + 3 * REC, 128)), shape((RIM + 3 * REC, 128))),
        in_specs=[VMEM] * 5,
        out_specs=(VMEM,) * 3,
        compiler_params=params(8),
        cost_estimate=cost(0, 2),
        name="edge",
    )(below, above, first, last, moved)


def shift_kernel(facts, hist, new_hist, head, buf, out, sems, osems):
    ins = [pltpu.make_async_copy(hist.at[c], buf.at[c], sems.at[c]) for c in range(3)]
    for copy in ins:
        copy.start()
    keep = facts[40:41, :]
    top = rows_of((H, 128)) == 0
    outs = [pltpu.make_async_copy(out.at[c], new_hist.at[c], osems.at[c]) for c in range(3)]
    for c in range(3):
        ins[c].wait()
        for k in range(NB // 128):
            lanes = slice(128 * k, 128 * k + 128)
            out[c, :, lanes] = jnp.where(top, 0.0, pltpu.roll(buf[c, :, lanes], 1, 0)) * keep[:, lanes]
        outs[c].start()
        head[c] = out[c, 0:8, :]
    for copy in outs:
        copy.wait()


def shifted(facts, hist):
    return pl.pallas_call(
        shift_kernel,
        out_shape=(shape((3, H, NB)), shape((3, 8, NB))),
        in_specs=[VMEM, HBM],
        out_specs=(HBM, VMEM),
        scratch_shapes=[
            pltpu.VMEM((3, H, NB), f32),
            pltpu.VMEM((3, H, NB), f32),
            pltpu.SemaphoreType.DMA((3,)),
            pltpu.SemaphoreType.DMA((3,)),
        ],
        compiler_params=params(16),
        cost_estimate=cost(1_000_000, 6),
        name="shifted",
    )(facts, *outside(hist))


def flow_at(facts, high, low, stacked, ya, yb, wh, wl):
    n = facts.shape[1]
    base = facts[0:3, :].astype(jnp.int32)
    wx = [w[0:1] for w in basis(facts[8:9, :])]
    wy = [w[0:1] for w in basis(facts[9:10, :])]
    wz = [w[0:1] for w in basis(facts[10:11, :])]
    bx, by, bz = base[0:1], base[1:2], base[2:3]
    along_x = spread(rows_of((CX, n)) - bx + 1, wx)
    along_y = spread(rows_of((CY, n)) - by + 1, wy)
    along_z = spread((rows_of((NZ, n)) - bz + 1) & (NZ - 1), wz)
    for z in range(NZ):
        h, l = split(along_x * along_z[z : z + 1, :])
        wh[z * CX : (z + 1) * CX, :n] = h
        wl[z * CX : (z + 1) * CX, :n] = l
    r = rows_of((2 * NZ, n))
    pair_z = spread(((r >> 1) - bz + 1) & (NZ - 1), wz)
    side = jnp.concatenate(
        [pair_z * spread((r & 1) - 2 - bx + 1, wx), pair_z * spread((r & 1) + CX - bx + 1, wx)], axis=0
    )
    h, l = split(side)
    side = jnp.concatenate([h, h, l, jnp.zeros((64, n), bf16)], axis=0)
    w_h, w_l = wh[:, :n], wl[:, :n]
    total = mul(high[...], w_h) + mul(low[...], w_h) + mul(high[...], w_l) + mul(stacked[...], side)
    fluid = [
        jnp.sum(total[c * CY : (c + 1) * CY, :] * along_y, axis=0, keepdims=True) for c in range(NF)
    ]
    inner = jnp.concatenate(
        [
            jnp.concatenate([y[16 * k : 16 * k + 16, :] for k in range(INNER // 128)], axis=1)
            for y in (ya, yb)
        ],
        axis=0,
    )
    inner_h, inner_l = split(inner)
    outer = jnp.concatenate([ya[RIM - 16 : RIM, :], yb[RIM - 16 : RIM, :]], axis=0)
    outer_h = outer.astype(bf16).astype(f32)
    outer = jnp.concatenate([outer_h + pltpu.roll(outer - outer_h, 64, 1), outer_h], axis=1).astype(bf16)
    rim = mul(inner_h, w_h) + mul(inner_l, w_h) + mul(inner_h, w_l) + mul(outer, side)
    extra = jnp.zeros((8, n), f32)
    for k, y in enumerate((-2, -1, CY, CY + 1)):
        extra = extra + rim[8 * k : 8 * k + 8, :] * spread(y - by + 1, wy)
    u = jnp.concatenate(fluid[0:3], axis=0) + extra[0:3]
    a = jnp.concatenate(fluid[3:6], axis=0) + extra[3:6]
    return u, a


def advance(facts, u, a):
    frac, speed, tail, keep = facts[16:19, :], facts[24:27, :], facts[32:35, :], facts[40:41, :]

    def rate(v):
        return 3.0 * a + (u - v) / relax_tau + basset_coef * (u - v + tail)

    v1 = speed + step_dt * rate(speed)
    v2 = 0.75 * speed + 0.25 * (v1 + step_dt * rate(v1))
    vn = speed / 3.0 + 2.0 / 3.0 * (v2 + step_dt * rate(v2))
    posn = frac + step_dt * (speed / 6.0 + v1 / 6.0 + 2.0 * v2 / 3.0)
    return vn * keep, posn * keep, (u - vn) * keep


def leaving_kernel(facts, high, low, stacked, ya, yb, moved, fore, back, wh, wl):
    u, a = flow_at(facts, high, low, stacked, ya, yb, wh, wl)
    vn, posn, recent = advance(facts, u, a)
    for out in (fore, back):
        out[0:16, :] = jnp.zeros((16, SLOTS), f32)
        out[0:3, :] = vn
        out[3:6, :] = posn
        out[6:9, :] = recent

    def here(ref, k):
        return ref[RIM + REC * k : RIM + REC * k + REC, :]

    fore[16 : 16 + REC, :] = here(yb, 2)
    fore[16 + REC : 16 + 2 * REC, :] = moved[6].reshape(REC, 128)
    fore[16 + 2 * REC : 16 + 3 * REC, :] = here(ya, 2)
    back[16 : 16 + REC, :] = here(yb, 0)
    back[16 + REC : 16 + 2 * REC, :] = moved[1].reshape(REC, 128)
    back[16 + 2 * REC : 16 + 3 * REC, :] = here(ya, 0)


def leaving(facts, high, low, stacked, ya, yb, moved):
    return pl.pallas_call(
        leaving_kernel,
        out_shape=(shape((16 + 3 * REC, SLOTS)),) * 2,
        in_specs=[VMEM] * 7,
        out_specs=(VMEM,) * 2,
        scratch_shapes=[pltpu.VMEM((INNER, SLOTS), bf16)] * 2,
        compiler_params=params(16),
        cost_estimate=cost(1_000_000_000, 4),
        name="leaving",
    )(facts, high, low, stacked, ya, yb, moved)


def staying_kernel(start, facts, high, low, stacked, ya, yb, head, *refs):
    vel, pos, hist, wh, wl, vbuf, pbuf, rows, sems = refs[-9:]
    tiles = rows.shape[2] // LANES
    for t in range(tiles):
        lanes = slice(LANES * t, LANES * t + LANES)
        source = slice(start + LANES * t, start + LANES * t + LANES)
        mine = facts[:, source]
        u, a = flow_at(mine, high, low, stacked, ya, yb, wh.at[t], wl.at[t])
        vn, posn, recent = advance(mine, u, a)
        vbuf[:, lanes] = vn
        pbuf[:, lanes] = posn
        for c in range(3):
            rows[c, :, lanes] = head[c, :, source]
            rows[c, 0:1, lanes] = recent[c : c + 1]
    span = pl.ds(start, LANES * tiles)
    copies = [
        pltpu.make_async_copy(vbuf, vel.at[:, span], sems.at[0]),
        pltpu.make_async_copy(pbuf, pos.at[:, span], sems.at[1]),
        pltpu.make_async_copy(rows, hist.at[:, pl.ds(0, 8), span], sems.at[2]),
    ]
    for copy in copies:
        copy.start()
    for copy in copies:
        copy.wait()


def staying(start, size, facts, high, low, stacked, ya, yb, head, filled):
    return pl.pallas_call(
        functools.partial(staying_kernel, start),
        out_shape=(shape((3, NB)), shape((3, NB)), shape((3, H, NB))),
        in_specs=[VMEM] * 7 + [HBM] * len(filled),
        out_specs=(HBM,) * 3,
        scratch_shapes=[
            pltpu.VMEM((size // LANES, INNER, LANES), bf16),
            pltpu.VMEM((size // LANES, INNER, LANES), bf16),
            pltpu.VMEM((3, size), f32),
            pltpu.VMEM((3, size), f32),
            pltpu.VMEM((3, 8, size), f32),
            pltpu.SemaphoreType.DMA((3,)),
        ],
        input_output_aliases={7 + k: 3 - len(filled) + k for k in range(len(filled))},
        compiler_params=params(24),
        cost_estimate=cost(6_000_000_000 * size // NB, 4),
        name="staying_%d" % start,
    )(facts, high, low, stacked, ya, yb, head, *filled)


def mix_kernel(own, fore, back, out):
    which = lax.broadcasted_iota(jnp.int32, (16, SLOTS), 1) // CAP
    out[...] = jnp.where(which < 3, back[0:16, :], jnp.where(which < 5, own[0:16, :], fore[0:16, :]))


def mix(own, fore, back):
    return pl.pallas_call(
        mix_kernel,
        out_shape=shape((16, SLOTS)),
        in_specs=[VMEM] * 3,
        out_specs=VMEM,
        compiler_params=params(4),
        cost_estimate=cost(0, 0.1),
        name="mix",
    )(own, fore, back)


def land_kernel(up, down, fore, back, ya, yb, state, record):
    which = lax.broadcasted_iota(jnp.int32, (16, SLOTS), 1) // CAP
    side = jnp.where(which == 1, back[0:16, :], fore[0:16, :])
    upward = (which == 2) | (which == 4) | (which == 7)
    landed = jnp.where((which == 1) | (which == 6), side, jnp.where(upward, up[...], down[...]))
    turned = jnp.concatenate([landed, jnp.zeros((SLOTS - 16, SLOTS), f32)], axis=0).T
    newest = lax.broadcasted_iota(jnp.int32, (CAP, 128), 1) == 0
    places = {3: (yb, RIM + REC), 4: (ya, RIM + REC)}
    for k in range(3):
        places[FORE[k]] = (fore, 16 + REC * k)
        places[BACK[k]] = (back, 16 + REC * k)
    for d in range(8):
        moved = pltpu.roll(landed, SLOTS - CAP * d, 1) if d else landed
        for r in range(6):
            state[r, d : d + 1, :] = moved[r : r + 1, :CAP]
        ref, base = places[d]
        for c in range(3):
            fresh = turned[CAP * d : CAP * d + CAP, 6 + c : 7 + c]
            old = ref[base + CAP * c : base + CAP * c + CAP, :]
            record[d, c, :, 0:128] = jnp.where(newest, fresh, old)
            record[d, c, :, 128:256] = ref[base + REC // 2 + CAP * c : base + REC // 2 + CAP * c + CAP, :]


def land(up, down, fore, back, ya, yb):
    return pl.pallas_call(
        land_kernel,
        out_shape=(shape((6, 8, CAP)), shape((8, 3, CAP, H))),
        in_specs=[VMEM] * 6,
        out_specs=(VMEM,) * 2,
        compiler_params=params(8),
        cost_estimate=cost(0, 1),
        name="land",
    )(up, down, fore, back, ya, yb)


def on_device(flow, cell, shift, frac, speed, hist, live, mig_slots, mig_count):
    below = from_behind(flow[:, :, CX - 2 :, :].reshape(NF * NZ * 2, CY), "gx", 1)
    above = from_behind(flow[:, :, :2, :].reshape(NF * NZ * 2, CY), "gx", -1)
    high, low, first, last, facts, moved, gone = prepare(
        live, flow.reshape(NF, INNER, CY), hist, cell, shift, frac, speed, mig_slots, mig_count
    )
    stacked, up, down = edge(below, above, first, last, moved)
    ya = from_behind(up, "gy", 1)
    yb = from_behind(down, "gy", -1)
    new_hist, head = shifted(facts, hist)
    fore, back = leaving(gone, high, low, stacked, ya, yb, moved)
    own = fore
    fore = from_behind(fore, "gx", 1)
    back = from_behind(back, "gx", -1)
    halves = (facts, high, low, stacked, ya, yb, head)
    filled = staying(0, 512, *halves, (new_hist,))
    late = mix(own, fore, back)
    up = from_behind(late, "gy", 1)
    down = from_behind(late, "gy", -1)
    vel, pos, new_hist = staying(512, 512, *halves, filled)
    state, record = land(up, down, fore, back, ya, yb)
    return vel, pos, new_hist, jnp.transpose(state, (1, 0, 2)), jnp.transpose(record, (0, 1, 3, 2))


def solution(mesh):
    both = ("gx", "gy")
    return jax.shard_map(
        on_device,
        mesh=mesh,
        in_specs=(
            P(None, None, "gx", "gy"),
            P(None, both),
            P(None, both),
            P(None, both),
            P(None, both),
            P(None, None, both),
            P(both),
            P(both, None, None),
            P(both, None),
        ),
        out_specs=(P(None, both), P(None, both), P(None, None, both), P(None, None, both), P(None, None, None, both)),
        check_vma=False,
    )
```

```python
import functools

import jax
import jax.numpy as jnp
from jax import lax
from jax.experimental import pallas as pl
from jax.experimental.pallas import tpu as pltpu
from jax.sharding import PartitionSpec as P

step_dt = 0.1
relax_tau = 0.5
basset_coef = 0.3

CX, CY, NZ, NB, CAP, H = 64, 128, 16, 1024, 16, 256
NF = 6
SLOTS = 8 * CAP
LANES = 256
f32 = jnp.float32
bf16 = jnp.bfloat16
VMEM = pl.BlockSpec(memory_space=pltpu.VMEM)
HBM = pl.BlockSpec(memory_space=pltpu.HBM)
SMEM = pl.BlockSpec(memory_space=pltpu.SMEM)
INNER = NZ * CX
WIDE = INNER + 128
BODY = NF * CY
TALL = BODY + 32
REC = 2 * 3 * CAP
FIRST_TILES = 2


def shape(dims, dtype=f32):
    return jax.ShapeDtypeStruct(dims, dtype)


def split(value):
    high = value.astype(bf16)
    return high, (value - high.astype(f32)).astype(bf16)


def mul(a, b):
    return jnp.dot(a, b, preferred_element_type=f32)


def rows_of(dims):
    return lax.broadcasted_iota(jnp.int32, dims, 0)


def from_behind(value, axis, steps):
    count = lax.axis_size(axis)
    return lax.ppermute(value, axis, [(k, (k + steps) % count) for k in range(count)])


def params(megabytes):
    return pltpu.CompilerParams(vmem_limit_bytes=megabytes << 20)


def outside(*arrays):
    return [pltpu.with_memory_space_constraint(x, pltpu.HBM) for x in arrays]


def cost(flops, megabytes):
    return pl.CostEstimate(flops=flops, bytes_accessed=int(megabytes * (1 << 20)), transcendentals=0)


def basis(s):
    return (
        -s * (s - 1.0) * (s - 2.0) / 6.0,
        (s + 1.0) * (s - 1.0) * (s - 2.0) / 2.0,
        -(s + 1.0) * s * (s - 2.0) / 2.0,
        (s + 1.0) * s * (s - 1.0) / 6.0,
    )


def spread(offset, weights):
    out = jnp.zeros(offset.shape, f32)
    for node, weight in enumerate(weights):
        out = jnp.where(offset == node, weight, out)
    return out


def call(kernel, name, out_shape, in_specs, out_specs, work, scratch=(), limit=16, aliases=None):
    return pl.pallas_call(
        kernel,
        out_shape=out_shape,
        in_specs=in_specs,
        out_specs=out_specs,
        scratch_shapes=scratch,
        input_output_aliases=aliases or {},
        compiler_params=params(limit),
        cost_estimate=cost(*work),
        name=name,
    )


def turn_kernel(field, high, low, first, last, left, right, buf, sems):
    copies = [pltpu.make_async_copy(field.at[c], buf.at[c], sems.at[c]) for c in range(NF)]
    for copy in copies:
        copy.start()
    first[...] = jnp.zeros(first.shape, f32)
    last[...] = jnp.zeros(last.shape, f32)
    for c in range(NF):
        copies[c].wait()
        for z in range(NZ):
            row = 2 * (NZ * c + z)
            left[row : row + 2, :] = buf[c, CX * z : CX * z + 2, :]
            right[row : row + 2, :] = buf[c, CX * z + CX - 2 : CX * z + CX, :]
        turned = buf[c].T
        h, l = split(turned)
        high[c * CY : (c + 1) * CY, :] = h
        low[c * CY : (c + 1) * CY, :] = l
        for i in range(2):
            first[8 * i + c : 8 * i + c + 1, :] = turned[i : i + 1, :]
            last[8 * i + c : 8 * i + c + 1, :] = turned[CY - 2 + i : CY - 1 + i, :]


def turn(field):
    return call(
        turn_kernel,
        "turn",
        (
            shape((TALL, INNER), bf16),
            shape((TALL, INNER), bf16),
            shape((16, INNER)),
            shape((16, INNER)),
            shape((2 * NZ * NF, CY)),
            shape((2 * NZ * NF, CY)),
        ),
        [HBM],
        (VMEM,) * 6,
        (0, 6),
        [pltpu.VMEM((NF, INNER, CY), f32), pltpu.SemaphoreType.DMA((NF,))],
    )(*outside(field))


def pick(value, choose):
    a = value.astype(bf16)
    rest = value - a.astype(f32)
    b = rest.astype(bf16)
    c = (rest - b.astype(f32)).astype(bf16)
    return mul(a, choose) + mul(b, choose) + mul(c, choose)


def gather_kernel(live, hist, cell, shift, frac, speed, slots, counts_in, facts, gone, choose, ibuf, vbuf, sbuf, counts, sems):
    pairs = (
        (cell, ibuf.at[0]),
        (shift, ibuf.at[1]),
        (frac, vbuf.at[0]),
        (speed, vbuf.at[1]),
        (slots, sbuf),
        (counts_in, counts),
    )
    small = [pltpu.make_async_copy(a, b, sems.at[k]) for k, (a, b) in enumerate(pairs)]
    for copy in small:
        copy.start()
    facts[...] = jnp.zeros(facts.shape, f32)
    karg = (rows_of((H, 128)) + 1).astype(f32)
    quad = jnp.sqrt(karg + 1.0) - jnp.sqrt(karg)
    for c in range(3):
        for k in range(NB // 128):
            lanes = slice(128 * k, 128 * k + 128)
            facts[32 + c : 33 + c, lanes] = jnp.sum(hist[c, :, lanes] * quad, axis=0, keepdims=True)
    for copy in small:
        copy.wait()
    lane = lax.broadcasted_iota(jnp.int32, (1, SLOTS), 1)
    used = jnp.zeros((1, SLOTS), f32)
    for d in range(8):
        used = jnp.where((lane >= d * CAP) & (lane < d * CAP + counts[0, d]), 1.0, used)
    facts[0:3, :] = (ibuf[0] + ibuf[1]).astype(f32)
    facts[8:11, :] = vbuf[0] - ibuf[1].astype(f32)
    facts[16:19, :] = vbuf[0]
    facts[24:27, :] = vbuf[1]
    facts[40:41, :] = (lax.broadcasted_iota(jnp.int32, (1, NB), 1) < live[0]).astype(f32)
    listed = jnp.concatenate([sbuf[0].astype(f32), jnp.zeros((8, SLOTS - CAP), f32)], axis=1)
    place = jnp.zeros((1, SLOTS), f32)
    for d in range(8):
        row = listed[d : d + 1, :]
        place = place + (pltpu.roll(row, d * CAP, 1) if d else row)
    place = jnp.where(used > 0.0, place, -1.0).astype(jnp.int32)
    chosen = jnp.where(lax.broadcasted_iota(jnp.int32, (NB, SLOTS), 0) == place, 1.0, 0.0).astype(bf16)
    choose[...] = chosen
    gone[...] = pick(facts[...], chosen)
    gone[40:41, :] = used


def gather(live, hist, *arrays):
    return call(
        gather_kernel,
        "gather",
        (shape((48, NB)), shape((48, SLOTS)), shape((NB, SLOTS), bf16)),
        [SMEM, VMEM] + [HBM] * 6,
        (VMEM,) * 3,
        (50_000_000, 4),
        [
            pltpu.VMEM((2, 3, NB), jnp.int32),
            pltpu.VMEM((2, 3, NB), f32),
            pltpu.VMEM((1, 8, CAP), jnp.int32),
            pltpu.SMEM((1, 8), jnp.int32),
            pltpu.SemaphoreType.DMA((6,)),
        ],
    )(live, hist, *outside(*arrays))


def edge_kernel(below, above, first, last, after, stacked, up, down):
    del after
    up[:, :INNER] = last[...]
    down[:, :INNER] = first[...]
    up[:, INNER:] = jnp.zeros((16, 128), f32)
    down[:, INNER:] = jnp.zeros((16, 128), f32)
    for c in range(NF):
        block = jnp.concatenate(
            [below[32 * c : 32 * c + 32, :], above[32 * c : 32 * c + 32, :], jnp.zeros((64, CY), f32)], axis=0
        )
        turned = block.T
        h = turned.astype(bf16).astype(f32)
        stacked[c * CY : (c + 1) * CY, :128] = (h + pltpu.roll(turned - h, 64, 1)).astype(bf16)
        stacked[c * CY : (c + 1) * CY, 128:] = h.astype(bf16)
        for i in range(2):
            row = slice(8 * i + c, 8 * i + c + 1)
            down[row, INNER:] = turned[i : i + 1, :]
            up[row, INNER:] = turned[CY - 2 + i : CY - 1 + i, :]


def edge(below, above, first, last, after):
    return call(
        edge_kernel,
        "edge",
        (shape((TALL, 256), bf16), shape((16, WIDE)), shape((16, WIDE))),
        [VMEM] * 5,
        (VMEM,) * 3,
        (0, 1),
    )(below, above, first, last, after)


def shift_kernel(facts, hist, choose, out, moved):
    top = rows_of((H, 128)) == 0
    newest = lax.broadcasted_iota(jnp.int32, (SLOTS, H), 1) == 0
    for c in range(3):
        for k in range(NB // 128):
            lanes = slice(128 * k, 128 * k + 128)
            out[c, :, lanes] = jnp.where(top, 0.0, pltpu.roll(hist[c, :, lanes], 1, 0)) * facts[40:41, lanes]
        chosen = jnp.where(newest, 0.0, pltpu.roll(pick(hist[c], choose[...]).T, 1, 1))
        for half in range(2):
            moved[:, half, c] = chosen[:, 128 * half : 128 * half + 128].reshape(8, CAP, 128)


def shifted(facts, hist, choose):
    return call(
        shift_kernel,
        "shifted",
        (shape((3, H, NB)), shape((8, 2, 3, CAP, 128))),
        [VMEM] * 3,
        (VMEM,) * 2,
        (600_000_000, 7),
    )(facts, hist, choose)


def weigh(facts, wh, wl):
    n = facts.shape[1]
    base = facts[0:3, :].astype(jnp.int32)
    wx = basis(facts[8:9, :])
    wy = basis(facts[9:10, :])
    wz = basis(facts[10:11, :])
    bx, by, bz = base[0:1], base[1:2], base[2:3]
    along_x = spread(rows_of((CX, n)) - bx + 1, wx)
    along_y = spread(rows_of((CY, n)) - by + 1, wy)
    along_z = spread((rows_of((NZ, n)) - bz + 1) & (NZ - 1), wz)
    for z in range(NZ):
        h, l = split(along_x * along_z[z : z + 1, :])
        wh[z * CX : (z + 1) * CX, :] = h
        wl[z * CX : (z + 1) * CX, :] = l
    r = rows_of((2 * NZ, n))
    pair_z = spread(((r >> 1) - bz + 1) & (NZ - 1), wz)
    side = jnp.concatenate(
        [pair_z * spread((r & 1) - 2 - bx + 1, wx), pair_z * spread((r & 1) + CX - bx + 1, wx)], axis=0
    )
    h, l = split(side)
    side = jnp.concatenate([h, h, l, jnp.zeros((64, n), bf16)], axis=0)
    return side, along_y, by, wy


def body_sum(total, along_y):
    fluid = [jnp.sum(total[c * CY : (c + 1) * CY, :] * along_y, axis=0, keepdims=True) for c in range(NF)]
    return jnp.concatenate(fluid[0:3], axis=0), jnp.concatenate(fluid[3:6], axis=0)


def rim_sum(total, by, wy):
    extra = jnp.zeros((8, total.shape[1]), f32)
    for k, y in enumerate((-2, -1, CY, CY + 1)):
        extra = extra + total[8 * k : 8 * k + 8, :] * spread(y - by + 1, wy)
    return extra[0:3], extra[3:6]


def advance(facts, u, a):
    frac, speed, tail, keep = facts[16:19, :], facts[24:27, :], facts[32:35, :], facts[40:41, :]

    def rate(v):
        return 3.0 * a + (u - v) / relax_tau + basset_coef * (u - v + tail)

    v1 = speed + step_dt * rate(speed)
    v2 = 0.75 * speed + 0.25 * (v1 + step_dt * rate(v1))
    vn = speed / 3.0 + 2.0 / 3.0 * (v2 + step_dt * rate(v2))
    posn = frac + step_dt * (speed / 6.0 + v1 / 6.0 + 2.0 * v2 / 3.0)
    return vn * keep, posn * keep, (u - vn) * keep


def apply(high, low, stacked, wh, wl, side):
    return mul(high, wh[...]) + mul(low, wh[...]) + mul(high, wl[...]) + mul(stacked, side)


def leaving_kernel(facts, high, low, stacked, moved, part, wh, wl, side, fore, back):
    edges, along_y, _, _ = weigh(facts, wh, wl)
    side[...] = edges
    rows = slice(0, BODY)
    u, a = body_sum(apply(high[rows, :], low[rows, :], stacked[rows, :], wh, wl, edges), along_y)
    part[0:3, :] = u
    part[8:11, :] = a
    for out, base in ((fore, 5), (back, 0)):
        for k in range(3):
            out[16 + REC * k : 16 + REC * k + REC, :] = moved[base + k].reshape(REC, 128)


def leaving(facts, high, low, stacked, moved):
    return call(
        leaving_kernel,
        "leaving",
        (
            shape((16, SLOTS)),
            shape((INNER, SLOTS), bf16),
            shape((INNER, SLOTS), bf16),
            shape((256, SLOTS), bf16),
            shape((16 + 3 * REC, SLOTS)),
            shape((16 + 3 * REC, SLOTS)),
        ),
        [VMEM] * 5,
        (VMEM,) * 6,
        (1_000_000_000, 4),
    )(facts, high, low, stacked, moved)


def finish_kernel(facts, part, wh, wl, side, ya, yb, *refs):
    high, low, stacked, fore, back = refs[5:]
    for k, y in enumerate((ya, yb)):
        rows = slice(BODY + 16 * k, BODY + 16 * k + 16)
        high[rows, :], low[rows, :] = split(y[:, :INNER])
        outer = y[:, INNER:]
        h = outer.astype(bf16).astype(f32)
        stacked[rows, :128] = (h + pltpu.roll(outer - h, 64, 1)).astype(bf16)
        stacked[rows, 128:] = h.astype(bf16)
    rows = slice(BODY, TALL)
    total = apply(high[rows, :], low[rows, :], stacked[rows, :], wh, wl, side[...])
    by = facts[1:2, :].astype(jnp.int32)
    u, a = rim_sum(total, by, basis(facts[9:10, :]))
    vn, posn, recent = advance(facts, part[0:3, :] + u, part[8:11, :] + a)
    for out in (fore, back):
        out[0:16, :] = jnp.zeros((16, SLOTS), f32)
        out[0:3, :] = vn
        out[3:6, :] = posn
        out[6:9, :] = recent


def finish(facts, part, wh, wl, side, ya, yb, *filled):
    return call(
        finish_kernel,
        "finish",
        tuple(shape(x.shape, x.dtype) for x in filled),
        [VMEM] * 12,
        (VMEM,) * 5,
        (60_000_000, 1),
        aliases={7 + k: k for k in range(5)},
    )(facts, part, wh, wl, side, ya, yb, *filled)


def staying_kernel(tiles, facts, high, low, stacked, *refs):
    if len(refs) == 7:
        past, vel, pos, recent, new_hist, weights, sem = refs
        copy = pltpu.make_async_copy(past, new_hist, sem)
        copy.start()
    else:
        vel, pos, recent, weights = refs
        copy = None
    for k, t in enumerate(tiles):
        lanes = slice(LANES * k, LANES * k + LANES)
        mine = facts[:, LANES * t : LANES * t + LANES]
        wh, wl = weights.at[k, 0], weights.at[k, 1]
        side, along_y, by, wy = weigh(mine, wh, wl)
        total = apply(high[...], low[...], stacked[...], wh, wl, side)
        u, a = body_sum(total, along_y)
        eu, ea = rim_sum(total[BODY:, :], by, wy)
        u, a = u + eu, a + ea
        vel[:, lanes], pos[:, lanes], recent[:, lanes] = advance(mine, u, a)
    if copy is not None:
        copy.wait()


def staying(tiles, facts, high, low, stacked, past=None):
    n = len(tiles)
    weights = pltpu.VMEM((n, 2, INNER, LANES), bf16)
    sole = (shape((3, LANES * n)),) * 3
    kernel = functools.partial(staying_kernel, tiles)
    work = (1_500_000_000 * n, 4)
    if past is None:
        return call(kernel, "staying_b", sole, [VMEM] * 4, (VMEM,) * 3, work, [weights])(facts, high, low, stacked)
    return call(
        kernel,
        "staying_a",
        sole + (shape((3, H, NB)),),
        [VMEM] * 5,
        (VMEM,) * 3 + (HBM,),
        work,
        [weights, pltpu.SemaphoreType.DMA],
    )(facts, high, low, stacked, past)


def mix_kernel(own, fore, back, moved, after, up, down):
    del after
    which = lax.broadcasted_iota(jnp.int32, (16, SLOTS), 1) // CAP
    late = jnp.where(which < 3, back[0:16, :], jnp.where(which < 5, own[0:16, :], fore[0:16, :]))
    for out, parts in (
        (up, (back[16 + 2 * REC : 16 + 3 * REC, :], moved[4].reshape(REC, 128), fore[16 + 2 * REC : 16 + 3 * REC, :])),
        (down, (back[16 : 16 + REC, :], moved[3].reshape(REC, 128), fore[16 : 16 + REC, :])),
    ):
        out[0:16, :] = late
        for k in range(3):
            out[16 + REC * k : 16 + REC * k + REC, :] = parts[k]


def mix(own, fore, back, moved, after):
    return call(
        mix_kernel, "mix", (shape((16 + 3 * REC, SLOTS)),) * 2, [VMEM] * 5, (VMEM,) * 2, (0, 0.5), limit=4
    )(own, fore, back, moved, after)


def land_kernel(up, down, fore, back, past, *refs):
    parts = refs[:6]
    hist_in, vel, pos, hist, state, record, rows, sbuf, rbuf, sems = refs[6:]
    del hist_in
    copies = []

    def send(src, dst):
        copy = pltpu.make_async_copy(src, dst, sems.at[len(copies)])
        copy.start()
        copies.append(copy)

    start = 0
    for k in range(2):
        v, p, recent = parts[3 * k : 3 * k + 3]
        size = v.shape[1]
        send(v, vel.at[:, pl.ds(start, size)])
        send(p, pos.at[:, pl.ds(start, size)])
        span = slice(start, start + size)
        for c in range(3):
            rows[c, :, span] = past[c, 0:8, span]
            rows[c, 0:1, span] = recent[c : c + 1, :]
        start += size
    send(rows, hist.at[:, pl.ds(0, 8), :])
    which = lax.broadcasted_iota(jnp.int32, (16, SLOTS), 1) // CAP
    side = jnp.where(which == 1, back[0:16, :], fore[0:16, :])
    upward = (which == 2) | (which == 4) | (which == 7)
    landed = jnp.where((which == 1) | (which == 6), side, jnp.where(upward, up[0:16, :], down[0:16, :]))
    turned = jnp.concatenate([landed, jnp.zeros((SLOTS - 16, SLOTS), f32)], axis=0).T
    newest = lax.broadcasted_iota(jnp.int32, (CAP, 128), 1) == 0
    places = ((down, 0), (back, 1), (up, 0), (down, 1), (up, 1), (down, 2), (fore, 1), (up, 2))
    for d in range(8):
        moved = pltpu.roll(landed, SLOTS - CAP * d, 1) if d else landed
        for r in range(6):
            sbuf[r, d : d + 1, :] = moved[r : r + 1, :CAP]
        ref, base = places[d][0], 16 + REC * places[d][1]
        for c in range(3):
            fresh = turned[CAP * d : CAP * d + CAP, 6 + c : 7 + c]
            old = ref[base + CAP * c : base + CAP * c + CAP, :]
            rbuf[d, c, :, 0:128] = jnp.where(newest, fresh, old)
            rbuf[d, c, :, 128:256] = ref[base + REC // 2 + CAP * c : base + REC // 2 + CAP * c + CAP, :]
        send(rbuf.at[d], record.at[d])
    send(sbuf, state)
    for copy in copies:
        copy.wait()


def land(up, down, fore, back, past, parts, hist):
    return call(
        land_kernel,
        "land",
        (shape((3, NB)), shape((3, NB)), shape((3, H, NB)), shape((6, 8, CAP)), shape((8, 3, CAP, H))),
        [VMEM] * 11 + [HBM],
        (HBM,) * 5,
        (0, 1),
        [
            pltpu.VMEM((3, 8, NB), f32),
            pltpu.VMEM((6, 8, CAP), f32),
            pltpu.VMEM((8, 3, CAP, H), f32),
            pltpu.SemaphoreType.DMA((14,)),
        ],
        limit=8,
        aliases={11: 2},
    )(up, down, fore, back, past, *parts, hist)


def on_device(flow, cell, shift, frac, speed, hist, live, mig_slots, mig_count):
    high, low, first, last, left, right = turn(flow.reshape(NF, INNER, CY))
    below = from_behind(right, "gx", 1)
    above = from_behind(left, "gx", -1)
    facts, gone, choose = gather(live, hist, cell, shift, frac, speed, mig_slots, mig_count)
    past, moved = shifted(facts, hist, choose)
    stacked, up, down = edge(below, above, first, last, moved)
    ya = from_behind(up, "gy", 1)
    yb = from_behind(down, "gy", -1)
    part, wh, wl, side, own, opposite = leaving(gone, high, low, stacked, moved)
    high, low, stacked, own, opposite = finish(gone, part, wh, wl, side, ya, yb, high, low, stacked, own, opposite)
    fore = from_behind(own, "gx", 1)
    back = from_behind(opposite, "gx", -1)
    tiles = tuple(range(NB // LANES))
    *some, new_hist = staying(tiles[:FIRST_TILES], facts, high, low, stacked, past)
    up, down = mix(own, fore, back, moved, some[0])
    up = from_behind(up, "gy", 1)
    down = from_behind(down, "gy", -1)
    more = staying(tiles[FIRST_TILES:], facts, high, low, stacked)
    vel, pos, new_hist, state, record = land(up, down, fore, back, past, (*some, *more), new_hist)
    return vel, pos, new_hist, jnp.transpose(state, (1, 0, 2)), jnp.transpose(record, (0, 1, 3, 2))


def solution(mesh):
    both = ("gx", "gy")
    return jax.shard_map(
        on_device,
        mesh=mesh,
        in_specs=(
            P(None, None, "gx", "gy"),
            P(None, both),
            P(None, both),
            P(None, both),
            P(None, both),
            P(None, None, both),
            P(both),
            P(both, None, None),
            P(both, None),
        ),
        out_specs=(P(None, both), P(None, both), P(None, None, both), P(None, None, both), P(None, None, None, both)),
        check_vma=False,
    )
```

```python
import functools

import jax
import jax.numpy as jnp
from jax import lax
from jax.experimental import pallas as pl
from jax.experimental.pallas import tpu as pltpu
from jax.sharding import PartitionSpec as P

step_dt = 0.1
relax_tau = 0.5
basset_coef = 0.3

CX, CY, NZ, NB, CAP, H = 64, 128, 16, 1024, 16, 256
NF = 6
SLOTS = 8 * CAP
LANES = 256
f32 = jnp.float32
bf16 = jnp.bfloat16
VMEM = pl.BlockSpec(memory_space=pltpu.VMEM)
HBM = pl.BlockSpec(memory_space=pltpu.HBM)
SMEM = pl.BlockSpec(memory_space=pltpu.SMEM)
INNER = NZ * CX
WIDE = INNER + 128
BODY = NF * CY
TALL = BODY + 32
REC = 2 * 3 * CAP
FIRST_TILES = 3


def shape(dims, dtype=f32):
    return jax.ShapeDtypeStruct(dims, dtype)


def split(value):
    high = value.astype(bf16)
    return high, (value - high.astype(f32)).astype(bf16)


def mul(a, b):
    return jnp.dot(a, b, preferred_element_type=f32)


def rows_of(dims):
    return lax.broadcasted_iota(jnp.int32, dims, 0)


def from_behind(value, axis, steps):
    count = lax.axis_size(axis)
    return lax.ppermute(value, axis, [(k, (k + steps) % count) for k in range(count)])


def params(megabytes):
    return pltpu.CompilerParams(vmem_limit_bytes=megabytes << 20)


def outside(*arrays):
    return [pltpu.with_memory_space_constraint(x, pltpu.HBM) for x in arrays]


def cost(flops, megabytes):
    return pl.CostEstimate(flops=flops, bytes_accessed=int(megabytes * (1 << 20)), transcendentals=0)


def basis(s):
    return (
        -s * (s - 1.0) * (s - 2.0) / 6.0,
        (s + 1.0) * (s - 1.0) * (s - 2.0) / 2.0,
        -(s + 1.0) * s * (s - 2.0) / 2.0,
        (s + 1.0) * s * (s - 1.0) / 6.0,
    )


def spread(offset, weights):
    out = jnp.zeros(offset.shape, f32)
    for node, weight in enumerate(weights):
        out = jnp.where(offset == node, weight, out)
    return out


def call(kernel, name, out_shape, in_specs, out_specs, work, scratch=(), limit=16, aliases=None):
    return pl.pallas_call(
        kernel,
        out_shape=out_shape,
        in_specs=in_specs,
        out_specs=out_specs,
        scratch_shapes=scratch,
        input_output_aliases=aliases or {},
        compiler_params=params(limit),
        cost_estimate=cost(*work),
        name=name,
    )


def turn_kernel(field, high, low, first, last, left, right, buf, sems):
    copies = [pltpu.make_async_copy(field.at[c], buf.at[c], sems.at[c]) for c in range(NF)]
    for copy in copies:
        copy.start()
    first[...] = jnp.zeros(first.shape, f32)
    last[...] = jnp.zeros(last.shape, f32)
    for c in range(NF):
        copies[c].wait()
        for z in range(NZ):
            row = 2 * (NZ * c + z)
            left[row : row + 2, :] = buf[c, CX * z : CX * z + 2, :]
            right[row : row + 2, :] = buf[c, CX * z + CX - 2 : CX * z + CX, :]
        turned = buf[c].T
        h, l = split(turned)
        high[c * CY : (c + 1) * CY, :] = h
        low[c * CY : (c + 1) * CY, :] = l
        for i in range(2):
            first[8 * i + c : 8 * i + c + 1, :] = turned[i : i + 1, :]
            last[8 * i + c : 8 * i + c + 1, :] = turned[CY - 2 + i : CY - 1 + i, :]


def turn(field):
    return call(
        turn_kernel,
        "turn",
        (
            shape((TALL, INNER), bf16),
            shape((TALL, INNER), bf16),
            shape((16, INNER)),
            shape((16, INNER)),
            shape((2 * NZ * NF, CY)),
            shape((2 * NZ * NF, CY)),
        ),
        [HBM],
        (VMEM,) * 6,
        (0, 6),
        [pltpu.VMEM((NF, INNER, CY), f32), pltpu.SemaphoreType.DMA((NF,))],
    )(*outside(field))


def pick(value, choose):
    a = value.astype(bf16)
    rest = value - a.astype(f32)
    b = rest.astype(bf16)
    c = (rest - b.astype(f32)).astype(bf16)
    return mul(a, choose) + mul(b, choose) + mul(c, choose)


def gather_kernel(live, hist, cell, shift, frac, speed, slots, counts_in, facts, gone, choose, ibuf, vbuf, sbuf, counts, sems):
    pairs = (
        (cell, ibuf.at[0]),
        (shift, ibuf.at[1]),
        (frac, vbuf.at[0]),
        (speed, vbuf.at[1]),
        (slots, sbuf),
        (counts_in, counts),
    )
    small = [pltpu.make_async_copy(a, b, sems.at[k]) for k, (a, b) in enumerate(pairs)]
    for copy in small:
        copy.start()
    facts[...] = jnp.zeros(facts.shape, f32)
    karg = (rows_of((H, 128)) + 1).astype(f32)
    quad = jnp.sqrt(karg + 1.0) - jnp.sqrt(karg)
    for c in range(3):
        for k in range(NB // 128):
            lanes = slice(128 * k, 128 * k + 128)
            facts[32 + c : 33 + c, lanes] = jnp.sum(hist[c, :, lanes] * quad, axis=0, keepdims=True)
    for copy in small:
        copy.wait()
    lane = lax.broadcasted_iota(jnp.int32, (1, SLOTS), 1)
    used = jnp.zeros((1, SLOTS), f32)
    for d in range(8):
        used = jnp.where((lane >= d * CAP) & (lane < d * CAP + counts[0, d]), 1.0, used)
    facts[0:3, :] = (ibuf[0] + ibuf[1]).astype(f32)
    facts[8:11, :] = vbuf[0] - ibuf[1].astype(f32)
    facts[16:19, :] = vbuf[0]
    facts[24:27, :] = vbuf[1]
    facts[40:41, :] = (lax.broadcasted_iota(jnp.int32, (1, NB), 1) < live[0]).astype(f32)
    listed = jnp.concatenate([sbuf[0].astype(f32), jnp.zeros((8, SLOTS - CAP), f32)], axis=1)
    place = jnp.zeros((1, SLOTS), f32)
    for d in range(8):
        row = listed[d : d + 1, :]
        place = place + (pltpu.roll(row, d * CAP, 1) if d else row)
    place = jnp.where(used > 0.0, place, -1.0).astype(jnp.int32)
    chosen = jnp.where(lax.broadcasted_iota(jnp.int32, (NB, SLOTS), 0) == place, 1.0, 0.0).astype(bf16)
    choose[...] = chosen
    gone[...] = pick(facts[...], chosen)
    gone[40:41, :] = used


def gather(live, hist, *arrays):
    return call(
        gather_kernel,
        "gather",
        (shape((48, NB)), shape((48, SLOTS)), shape((NB, SLOTS), bf16)),
        [SMEM, VMEM] + [HBM] * 6,
        (VMEM,) * 3,
        (50_000_000, 4),
        [
            pltpu.VMEM((2, 3, NB), jnp.int32),
            pltpu.VMEM((2, 3, NB), f32),
            pltpu.VMEM((1, 8, CAP), jnp.int32),
            pltpu.SMEM((1, 8), jnp.int32),
            pltpu.SemaphoreType.DMA((6,)),
        ],
    )(live, hist, *outside(*arrays))


def edge_kernel(below, above, first, last, after, stacked, up, down):
    del after
    up[:, :INNER] = last[...]
    down[:, :INNER] = first[...]
    up[:, INNER:] = jnp.zeros((16, 128), f32)
    down[:, INNER:] = jnp.zeros((16, 128), f32)
    for c in range(NF):
        block = jnp.concatenate(
            [below[32 * c : 32 * c + 32, :], above[32 * c : 32 * c + 32, :], jnp.zeros((64, CY), f32)], axis=0
        )
        turned = block.T
        h = turned.astype(bf16).astype(f32)
        stacked[c * CY : (c + 1) * CY, :128] = (h + pltpu.roll(turned - h, 64, 1)).astype(bf16)
        stacked[c * CY : (c + 1) * CY, 128:] = h.astype(bf16)
        for i in range(2):
            row = slice(8 * i + c, 8 * i + c + 1)
            down[row, INNER:] = turned[i : i + 1, :]
            up[row, INNER:] = turned[CY - 2 + i : CY - 1 + i, :]


def edge(below, above, first, last, after):
    return call(
        edge_kernel,
        "edge",
        (shape((TALL, 256), bf16), shape((16, WIDE)), shape((16, WIDE))),
        [VMEM] * 5,
        (VMEM,) * 3,
        (0, 1),
    )(below, above, first, last, after)


def shift_kernel(facts, hist, choose, out, moved):
    top = rows_of((H, 128)) == 0
    newest = lax.broadcasted_iota(jnp.int32, (SLOTS, H), 1) == 0
    for c in range(3):
        for k in range(NB // 128):
            lanes = slice(128 * k, 128 * k + 128)
            out[c, :, lanes] = jnp.where(top, 0.0, pltpu.roll(hist[c, :, lanes], 1, 0)) * facts[40:41, lanes]
        chosen = jnp.where(newest, 0.0, pltpu.roll(pick(hist[c], choose[...]).T, 1, 1))
        for half in range(2):
            moved[:, half, c] = chosen[:, 128 * half : 128 * half + 128].reshape(8, CAP, 128)


def shifted(facts, hist, choose):
    return call(
        shift_kernel,
        "shifted",
        (shape((3, H, NB)), shape((8, 2, 3, CAP, 128))),
        [VMEM] * 3,
        (VMEM,) * 2,
        (600_000_000, 7),
    )(facts, hist, choose)


def weigh(facts, wh, wl):
    n = facts.shape[1]
    base = facts[0:3, :].astype(jnp.int32)
    wx = basis(facts[8:9, :])
    wy = basis(facts[9:10, :])
    wz = basis(facts[10:11, :])
    bx, by, bz = base[0:1], base[1:2], base[2:3]
    along_x = spread(rows_of((CX, n)) - bx + 1, wx)
    along_y = spread(rows_of((CY, n)) - by + 1, wy)
    along_z = spread((rows_of((NZ, n)) - bz + 1) & (NZ - 1), wz)
    for z in range(NZ):
        h, l = split(along_x * along_z[z : z + 1, :])
        wh[z * CX : (z + 1) * CX, :] = h
        wl[z * CX : (z + 1) * CX, :] = l
    r = rows_of((2 * NZ, n))
    pair_z = spread(((r >> 1) - bz + 1) & (NZ - 1), wz)
    side = jnp.concatenate(
        [pair_z * spread((r & 1) - 2 - bx + 1, wx), pair_z * spread((r & 1) + CX - bx + 1, wx)], axis=0
    )
    h, l = split(side)
    side = jnp.concatenate([h, h, l, jnp.zeros((64, n), bf16)], axis=0)
    return side, along_y, by, wy


def body_sum(total, along_y):
    fluid = [jnp.sum(total[c * CY : (c + 1) * CY, :] * along_y, axis=0, keepdims=True) for c in range(NF)]
    return jnp.concatenate(fluid[0:3], axis=0), jnp.concatenate(fluid[3:6], axis=0)


def rim_sum(total, by, wy):
    extra = jnp.zeros((8, total.shape[1]), f32)
    for k, y in enumerate((-2, -1, CY, CY + 1)):
        extra = extra + total[8 * k : 8 * k + 8, :] * spread(y - by + 1, wy)
    return extra[0:3], extra[3:6]


def advance(facts, u, a):
    frac, speed, tail, keep = facts[16:19, :], facts[24:27, :], facts[32:35, :], facts[40:41, :]

    def rate(v):
        return 3.0 * a + (u - v) / relax_tau + basset_coef * (u - v + tail)

    v1 = speed + step_dt * rate(speed)
    v2 = 0.75 * speed + 0.25 * (v1 + step_dt * rate(v1))
    vn = speed / 3.0 + 2.0 / 3.0 * (v2 + step_dt * rate(v2))
    posn = frac + step_dt * (speed / 6.0 + v1 / 6.0 + 2.0 * v2 / 3.0)
    return vn * keep, posn * keep, (u - vn) * keep


def apply(high, low, stacked, wh, wl, side):
    return mul(high, wh[...]) + mul(low, wh[...]) + mul(high, wl[...]) + mul(stacked, side)


def leaving_kernel(facts, high, low, stacked, moved, part, wh, wl, side, fore, back):
    edges, along_y, _, _ = weigh(facts, wh, wl)
    side[...] = edges
    rows = slice(0, BODY)
    u, a = body_sum(apply(high[rows, :], low[rows, :], stacked[rows, :], wh, wl, edges), along_y)
    part[0:3, :] = u
    part[8:11, :] = a
    for out, base in ((fore, 5), (back, 0)):
        for k in range(3):
            out[16 + REC * k : 16 + REC * k + REC, :] = moved[base + k].reshape(REC, 128)


def leaving(facts, high, low, stacked, moved):
    return call(
        leaving_kernel,
        "leaving",
        (
            shape((16, SLOTS)),
            shape((INNER, SLOTS), bf16),
            shape((INNER, SLOTS), bf16),
            shape((256, SLOTS), bf16),
            shape((16 + 3 * REC, SLOTS)),
            shape((16 + 3 * REC, SLOTS)),
        ),
        [VMEM] * 5,
        (VMEM,) * 6,
        (1_000_000_000, 4),
    )(facts, high, low, stacked, moved)


def finish_kernel(facts, part, wh, wl, side, ya, yb, *refs):
    high, low, stacked, fore, back = refs[5:]
    for k, y in enumerate((ya, yb)):
        rows = slice(BODY + 16 * k, BODY + 16 * k + 16)
        high[rows, :], low[rows, :] = split(y[:, :INNER])
        outer = y[:, INNER:]
        h = outer.astype(bf16).astype(f32)
        stacked[rows, :128] = (h + pltpu.roll(outer - h, 64, 1)).astype(bf16)
        stacked[rows, 128:] = h.astype(bf16)
    rows = slice(BODY, TALL)
    total = apply(high[rows, :], low[rows, :], stacked[rows, :], wh, wl, side[...])
    by = facts[1:2, :].astype(jnp.int32)
    u, a = rim_sum(total, by, basis(facts[9:10, :]))
    vn, posn, recent = advance(facts, part[0:3, :] + u, part[8:11, :] + a)
    for out in (fore, back):
        out[0:16, :] = jnp.zeros((16, SLOTS), f32)
        out[0:3, :] = vn
        out[3:6, :] = posn
        out[6:9, :] = recent


def finish(facts, part, wh, wl, side, ya, yb, *filled):
    return call(
        finish_kernel,
        "finish",
        tuple(shape(x.shape, x.dtype) for x in filled),
        [VMEM] * 12,
        (VMEM,) * 5,
        (60_000_000, 1),
        aliases={7 + k: k for k in range(5)},
    )(facts, part, wh, wl, side, ya, yb, *filled)


def staying_kernel(tiles, facts, high, low, stacked, *refs):
    if len(refs) == 7:
        past, vel, pos, recent, new_hist, weights, sem = refs
        copy = pltpu.make_async_copy(past, new_hist, sem)
        copy.start()
    else:
        vel, pos, recent, weights = refs
        copy = None
    for k, t in enumerate(tiles):
        lanes = slice(LANES * k, LANES * k + LANES)
        mine = facts[:, LANES * t : LANES * t + LANES]
        wh, wl = weights.at[k, 0], weights.at[k, 1]
        side, along_y, by, wy = weigh(mine, wh, wl)
        total = apply(high[...], low[...], stacked[...], wh, wl, side)
        u, a = body_sum(total, along_y)
        eu, ea = rim_sum(total[BODY:, :], by, wy)
        u, a = u + eu, a + ea
        vel[:, lanes], pos[:, lanes], recent[:, lanes] = advance(mine, u, a)
    if copy is not None:
        copy.wait()


def staying(tiles, facts, high, low, stacked, past=None):
    n = len(tiles)
    weights = pltpu.VMEM((n, 2, INNER, LANES), bf16)
    sole = (shape((3, LANES * n)),) * 3
    kernel = functools.partial(staying_kernel, tiles)
    work = (1_500_000_000 * n, 4)
    if past is None:
        return call(kernel, "staying_b", sole, [VMEM] * 4, (VMEM,) * 3, work, [weights])(facts, high, low, stacked)
    return call(
        kernel,
        "staying_a",
        sole + (shape((3, H, NB)),),
        [VMEM] * 5,
        (VMEM,) * 3 + (HBM,),
        work,
        [weights, pltpu.SemaphoreType.DMA],
    )(facts, high, low, stacked, past)


def mix_kernel(own, fore, back, moved, after, up, down):
    del after
    which = lax.broadcasted_iota(jnp.int32, (16, SLOTS), 1) // CAP
    late = jnp.where(which < 3, back[0:16, :], jnp.where(which < 5, own[0:16, :], fore[0:16, :]))
    for out, parts in (
        (up, (back[16 + 2 * REC : 16 + 3 * REC, :], moved[4].reshape(REC, 128), fore[16 + 2 * REC : 16 + 3 * REC, :])),
        (down, (back[16 : 16 + REC, :], moved[3].reshape(REC, 128), fore[16 : 16 + REC, :])),
    ):
        out[0:16, :] = late
        for k in range(3):
            out[16 + REC * k : 16 + REC * k + REC, :] = parts[k]


def mix(own, fore, back, moved, after):
    return call(
        mix_kernel, "mix", (shape((16 + 3 * REC, SLOTS)),) * 2, [VMEM] * 5, (VMEM,) * 2, (0, 0.5), limit=4
    )(own, fore, back, moved, after)


def land_kernel(up, down, fore, back, past, *refs):
    parts = refs[:6]
    hist_in, vel, pos, hist, state, record, rows, sbuf, rbuf, sems = refs[6:]
    del hist_in
    copies = []

    def send(src, dst):
        copy = pltpu.make_async_copy(src, dst, sems.at[len(copies)])
        copy.start()
        copies.append(copy)

    start = 0
    for k in range(2):
        v, p, recent = parts[3 * k : 3 * k + 3]
        size = v.shape[1]
        send(v, vel.at[:, pl.ds(start, size)])
        send(p, pos.at[:, pl.ds(start, size)])
        span = slice(start, start + size)
        for c in range(3):
            rows[c, :, span] = past[c, 0:8, span]
            rows[c, 0:1, span] = recent[c : c + 1, :]
        start += size
    send(rows, hist.at[:, pl.ds(0, 8), :])
    which = lax.broadcasted_iota(jnp.int32, (16, SLOTS), 1) // CAP
    side = jnp.where(which == 1, back[0:16, :], fore[0:16, :])
    upward = (which == 2) | (which == 4) | (which == 7)
    landed = jnp.where((which == 1) | (which == 6), side, jnp.where(upward, up[0:16, :], down[0:16, :]))
    turned = jnp.concatenate([landed, jnp.zeros((SLOTS - 16, SLOTS), f32)], axis=0).T
    newest = lax.broadcasted_iota(jnp.int32, (CAP, 128), 1) == 0
    places = ((down, 0), (back, 1), (up, 0), (down, 1), (up, 1), (down, 2), (fore, 1), (up, 2))
    for d in range(8):
        moved = pltpu.roll(landed, SLOTS - CAP * d, 1) if d else landed
        for r in range(6):
            sbuf[r, d : d + 1, :] = moved[r : r + 1, :CAP]
        ref, base = places[d][0], 16 + REC * places[d][1]
        for c in range(3):
            fresh = turned[CAP * d : CAP * d + CAP, 6 + c : 7 + c]
            old = ref[base + CAP * c : base + CAP * c + CAP, :]
            rbuf[d, c, :, 0:128] = jnp.where(newest, fresh, old)
            rbuf[d, c, :, 128:256] = ref[base + REC // 2 + CAP * c : base + REC // 2 + CAP * c + CAP, :]
        send(rbuf.at[d], record.at[d])
    send(sbuf, state)
    for copy in copies:
        copy.wait()


def land(up, down, fore, back, past, parts, hist):
    return call(
        land_kernel,
        "land",
        (shape((3, NB)), shape((3, NB)), shape((3, H, NB)), shape((6, 8, CAP)), shape((8, 3, CAP, H))),
        [VMEM] * 11 + [HBM],
        (HBM,) * 5,
        (0, 1),
        [
            pltpu.VMEM((3, 8, NB), f32),
            pltpu.VMEM((6, 8, CAP), f32),
            pltpu.VMEM((8, 3, CAP, H), f32),
            pltpu.SemaphoreType.DMA((14,)),
        ],
        limit=8,
        aliases={11: 2},
    )(up, down, fore, back, past, *parts, hist)


def on_device(flow, cell, shift, frac, speed, hist, live, mig_slots, mig_count):
    high, low, first, last, left, right = turn(flow.reshape(NF, INNER, CY))
    below = from_behind(right, "gx", 1)
    above = from_behind(left, "gx", -1)
    facts, gone, choose = gather(live, hist, cell, shift, frac, speed, mig_slots, mig_count)
    past, moved = shifted(facts, hist, choose)
    stacked, up, down = edge(below, above, first, last, moved)
    ya = from_behind(up, "gy", 1)
    yb = from_behind(down, "gy", -1)
    part, wh, wl, side, own, opposite = leaving(gone, high, low, stacked, moved)
    high, low, stacked, own, opposite = finish(gone, part, wh, wl, side, ya, yb, high, low, stacked, own, opposite)
    fore = from_behind(own, "gx", 1)
    back = from_behind(opposite, "gx", -1)
    tiles = tuple(range(NB // LANES))
    *some, new_hist = staying(tiles[:FIRST_TILES], facts, high, low, stacked, past)
    up, down = mix(own, fore, back, moved, some[0])
    up = from_behind(up, "gy", 1)
    down = from_behind(down, "gy", -1)
    more = staying(tiles[FIRST_TILES:], facts, high, low, stacked)
    vel, pos, new_hist, state, record = land(up, down, fore, back, past, (*some, *more), new_hist)
    return vel, pos, new_hist, jnp.transpose(state, (1, 0, 2)), jnp.transpose(record, (0, 1, 3, 2))


def solution(mesh):
    both = ("gx", "gy")
    return jax.shard_map(
        on_device,
        mesh=mesh,
        in_specs=(
            P(None, None, "gx", "gy"),
            P(None, both),
            P(None, both),
            P(None, both),
            P(None, both),
            P(None, None, both),
            P(both),
            P(both, None, None),
            P(both, None),
        ),
        out_specs=(P(None, both), P(None, both), P(None, None, both), P(None, None, both), P(None, None, None, both)),
        check_vma=False,
    )
```
